32 devices in a mesh: groups: 2 (over x), ctx: 16 (over z, y, core).
Axes of the slice: x: 2, y: 2, z: 4, core: 2. Of those that a mesh axis runs over, the one named last changes fastest.
Arguments:
- query_video: bfloat16 [12288, 1536], P(('groups', 'ctx')), parts along dimension 0, may hold values from -10 to 10
- key_video: bfloat16 [12288, 1536], P(('groups', 'ctx')), parts along dimension 0, may hold values from -5 to 5
- value_video: bfloat16 [12288, 1536], P(('groups', 'ctx')), parts along dimension 0, may hold values from -6 to 6
- query_text: bfloat16 [512, 1536], P(('groups', 'ctx')), parts along dimension 0, may hold values from -10 to 10
- key_text: bfloat16 [512, 1536], P(('groups', 'ctx')), parts along dimension 0, may hold values from -5 to 5
- value_text: bfloat16 [512, 1536], P(('groups', 'ctx')), parts along dimension 0, may hold values from -6 to 6
- key_tiles: int32 [32, 3], P(('groups', 'ctx')), parts along dimension 0, may hold values from 0 to 15, as said below
- tile_owner: int32 [32], P('groups'), parts along dimension 0, may hold values from 0 to 15, as said below
- text_count: int32 [2], P('groups'), parts along dimension 0, may hold values from 64 to 256
Outputs:
- video_out: bfloat16 [12288, 1536], P(('groups', 'ctx')), parts along dimension 0
- text_out: bfloat16 [512, 1536], P(('groups', 'ctx')), parts along dimension 0
The draws below stay inside these ranges and needn't reach their ends.
There are 2 independent parts, one for each index of `groups`. The reference program is written for one: setup_inputs(seed, part) draws one part's arguments, and reference() takes and returns one part's arrays. A program takes and returns all parts, laid end to end along the dimension named above; each array names one. Nothing has to cross between parts.
Inputs may be any that keep to these rules, and one draw needn't show every extreme that they name: `key_tiles`: each list names 3 different tiles, the query tile itself among them; every listed tile has a stored position whose device (position) is at most 2 away from the query tile's device, and every list names one exactly 2 away. `tile_owner`: A permutation of the tile numbers.
All inputs are finite; a program needn't handle non-finite values.
Results may differ from the reference program's by a relative error of at most 0.0032.
Values may be sent and summed in bfloat16 or wider, within the bound.
A program may use at most 384 MiB of HBM per device.

```python
import math
import jax
import jax.numpy as jnp
from jax import lax

TILE = 384
HEADS = 12
HD = 128
NB = 3
REACH = 2
TXT = 256
TPD = 1
TILES = 16
VID = 6144


def rough_rows(key, row_count, spread, limit):
    drawn = jax.random.normal(key, (row_count, HEADS * HD), jnp.float32)
    return jnp.clip(drawn * spread, -limit, limit)


def draw_query_video(key, part):
    rows_drawn = rough_rows(jax.random.fold_in(key, 1), VID, 2.5, 10.0)
    return rows_drawn.astype(jnp.bfloat16)


def draw_key_video(key, part):
    rows_drawn = rough_rows(jax.random.fold_in(key, 2), VID, 1.0, 5.0)
    return rows_drawn.astype(jnp.bfloat16)


def draw_query_text(key, part):
    rows_drawn = rough_rows(jax.random.fold_in(key, 4), TXT, 2.5, 10.0)
    return rows_drawn.astype(jnp.bfloat16)


def draw_key_text(key, part):
    rows_drawn = rough_rows(jax.random.fold_in(key, 5), TXT, 1.0, 5.0)
    return rows_drawn.astype(jnp.bfloat16)


def tile_layout(key):
    layout_key = jax.random.fold_in(key, 11)
    slot_ids = jnp.arange(TILES, dtype=jnp.int32)
    device_ids = slot_ids // TPD
    window_size = (2 * REACH + 1) * TPD
    window_steps = jnp.arange(window_size, dtype=jnp.int32)
    candidates = (device_ids[:, None] - REACH) * TPD + window_steps[None, :]
    inside = (candidates >= 0) & (candidates < TILES)
    random_part = jax.random.randint(layout_key, (TILES, window_size), 0, 4096, dtype=jnp.int32)
    ranking = random_part * window_size + window_steps[None, :]
    remote_partner = inside & (jnp.abs(candidates // TPD - device_ids[:, None]) == REACH)
    far_rank = jnp.where(remote_partner, ranking, -1)
    far_best = jnp.max(far_rank, axis=1, keepdims=True)
    ranking = jnp.where(remote_partner & (far_rank == far_best), ranking + 2 ** 24, ranking)
    ranking = jnp.where(candidates == slot_ids[:, None], ranking + 2 ** 25, ranking)
    ranking = jnp.where(inside, ranking, -2 ** 26)
    chosen = lax.top_k(ranking, NB)[1]
    picked_slots = jnp.take_along_axis(candidates, chosen, axis=1)
    spatial_order = jax.random.permutation(jax.random.fold_in(key, 12), TILES).astype(jnp.int32)
    owner_table = jnp.zeros((TILES,), jnp.int32).at[spatial_order].set(slot_ids)
    listed = spatial_order[picked_slots]
    return (listed.astype(jnp.int32), owner_table)


def draw_key_tiles(key, part):
    return tile_layout(key)[0]


def draw_tile_owner(key, part):
    return tile_layout(key)[1]


def levels(stream_key, extent, shards, low, largest):
    factor_of, own = 1.0, jax.random.fold_in(stream_key, 6)
    for dim, parts in shards:
        draws = jnp.exp(jax.random.uniform(jax.random.fold_in(own, dim), (parts,), jnp.float32, low / len(shards), largest / len(shards)))
        factor_of = factor_of * jnp.repeat(draws, extent[dim] // parts).reshape([-1 if axis == dim else 1 for axis in range(len(extent))])
    return factor_of


def normal_values(rng, shape, deviation, most, pieces=(), kind=jnp.bfloat16):
    values = deviation * jax.random.normal(rng, shape, jnp.float32)
    if pieces:
        values = values * levels(rng, shape, pieces, -0.22, 0.18)
    return jnp.clip(values, -most, most).astype(kind)


def setup_inputs(seed: int = 0, part: int = 0) -> dict:
    arg_keys = jax.random.split(jax.random.key(seed), 10)
    own_keys = jax.random.split(jax.random.fold_in(arg_keys[9], part), 10)
    query_video = draw_query_video(jax.random.fold_in(jax.random.fold_in(arg_keys[9], part), 71), part)
    key_video = draw_key_video(jax.random.fold_in(jax.random.fold_in(arg_keys[9], part), 71), part)
    value_video = normal_values(own_keys[2], (VID, HEADS * HD), 1.0, 6.0, ((0, 16),))
    query_text = draw_query_text(jax.random.fold_in(jax.random.fold_in(arg_keys[9], part), 71), part)
    key_text = draw_key_text(jax.random.fold_in(jax.random.fold_in(arg_keys[9], part), 71), part)
    value_text = normal_values(own_keys[5], (TXT, HEADS * HD), 1.0, 6.0, ((0, 16),))
    key_tiles = draw_key_tiles(jax.random.fold_in(jax.random.fold_in(arg_keys[9], part), 71), part)
    tile_owner = draw_tile_owner(jax.random.fold_in(jax.random.fold_in(arg_keys[9], part), 71), part)
    text_count = jax.random.randint(own_keys[8], (1,), TXT // 4, TXT + 1).astype(jnp.int32)
    return dict(query_video=query_video, key_video=key_video, value_video=value_video, query_text=query_text, key_text=key_text, value_text=value_text, key_tiles=key_tiles, tile_owner=tile_owner, text_count=text_count)


def rounded_copy(values):
    return lax.optimization_barrier(values.astype(jnp.bfloat16)).astype(jnp.float32)

def reference(query_video, key_video, value_video, query_text, key_text, value_text, key_tiles, tile_owner, text_count):
    feature_width = HEADS * HD
    inverse_root_dimension = 1.0 / math.sqrt(HD)
    text_ok = jnp.arange(TXT) < text_count[0]
    key_slots = tile_owner[key_tiles].astype(jnp.int32)
    key_grid = key_video.reshape(TILES, TILE, HEADS, HD)
    value_grid = value_video.reshape(TILES, TILE, HEADS, HD)
    text_keys = key_text.reshape(TXT, HEADS, HD).astype(jnp.float32)
    text_values = value_text.reshape(TXT, HEADS, HD).astype(jnp.float32)

    def one_tile(tile_data):
        query_tile, slot_list = tile_data
        adjacent_tile_lookups = key_grid[slot_list].reshape(NB * TILE, HEADS, HD).astype(jnp.float32)
        value_rows = value_grid[slot_list].reshape(NB * TILE, HEADS, HD).astype(jnp.float32)
        asking_token_array = query_tile.reshape(TILE, HEADS, HD).astype(jnp.float32)
        frame_affinity_array = jnp.einsum('qhd,khd->hqk', asking_token_array, adjacent_tile_lookups) * inverse_root_dimension
        wording_affinity_array = jnp.einsum('qhd,khd->hqk', asking_token_array, text_keys) * inverse_root_dimension
        wording_affinity_array = jnp.where(text_ok[None, None, :], wording_affinity_array, -jnp.inf)
        scores = jnp.concatenate([frame_affinity_array, wording_affinity_array], axis=-1)
        row_max = lax.optimization_barrier(jnp.max(scores, axis=-1, keepdims=True))
        weights = jnp.exp(scores - row_max)
        row_total = lax.optimization_barrier(jnp.sum(weights, axis=-1))
        rounded_scores = rounded_copy(weights)
        combined_value_rows = jnp.concatenate([value_rows, text_values], axis=0)
        output_tile = jnp.einsum('hqk,khd->qhd', rounded_scores, combined_value_rows)
        output_tile = output_tile / jnp.transpose(row_total)[:, :, None]
        return output_tile.reshape(TILE, feature_width).astype(jnp.bfloat16)
    video_out = lax.map(one_tile, (query_video.reshape(TILES, TILE, feature_width), key_slots))
    video_out = video_out.reshape(VID, feature_width)
    blocks = TILES // TPD
    video_block = TPD * TILE
    text_block = TXT // blocks
    text_query_heads = jnp.transpose(query_text.reshape(TXT, HEADS, HD), (1, 0, 2))
    key_block_heads = jnp.transpose(key_video.reshape(blocks, video_block, HEADS, HD), (2, 0, 1, 3))
    value_block_heads = jnp.transpose(value_video.reshape(blocks, video_block, HEADS, HD), (2, 0, 1, 3))
    text_key_heads = jnp.transpose(key_text.reshape(blocks, text_block, HEADS, HD), (2, 0, 1, 3))
    text_value_heads = jnp.transpose(value_text.reshape(blocks, text_block, HEADS, HD), (2, 0, 1, 3))
    block_ok = text_ok.reshape(blocks, text_block)

    def one_head(head_data):
        asking_token_array, adjacent_tile_lookups, value_rows, subtitle_lookup_entries, text_value_rows = head_data
        asking_token_array = asking_token_array.astype(jnp.float32)
        frame_affinity_array = jnp.einsum('pb,dmb->dpm', asking_token_array, adjacent_tile_lookups.astype(jnp.float32)) * inverse_root_dimension
        wording_affinity_array = jnp.einsum('pb,dmb->dpm', asking_token_array, subtitle_lookup_entries.astype(jnp.float32)) * inverse_root_dimension
        wording_affinity_array = jnp.where(block_ok[:, None, :], wording_affinity_array, -jnp.inf)
        scores = jnp.concatenate([frame_affinity_array, wording_affinity_array], axis=-1)
        block_max = lax.optimization_barrier(jnp.max(scores, axis=-1))
        weights = jnp.exp(scores - block_max[:, :, None])
        block_total = lax.optimization_barrier(jnp.sum(weights, axis=-1))
        rounded_scores = rounded_copy(weights)
        combined_value_rows = jnp.concatenate([value_rows, text_value_rows], axis=1).astype(jnp.float32)
        block_weight_sum = jnp.einsum('ywu,yuo->ywo', rounded_scores, combined_value_rows)
        overall_peak = lax.optimization_barrier(jnp.max(block_max, axis=0))
        factor = jnp.exp(block_max - overall_peak[None, :])
        text_total = lax.optimization_barrier(jnp.sum(block_total * factor, axis=0))
        text_acc = lax.optimization_barrier(jnp.sum(block_weight_sum * factor[:, :, None], axis=0))
        return text_acc / text_total[:, None]
    head_results = lax.map(one_head, (text_query_heads, key_block_heads, value_block_heads, text_key_heads, text_value_heads))
    text_out = jnp.transpose(head_results, (1, 0, 2)).reshape(TXT, feature_width).astype(jnp.bfloat16)
    return (video_out, text_out)
```

```python
import functools
import math

import jax
import jax.numpy as jnp
from jax import lax
from jax.experimental import pallas as pl
from jax.experimental.pallas import tpu as pltpu
from jax.sharding import PartitionSpec as P

TILE = 384
HD = 128
REACH = 2
CHUNK = 3
C2 = math.log2(math.e) / math.sqrt(HD)


def qk(q, k):
    return lax.dot_general(q, k, (((1,), (1,)), ((), ())), preferred_element_type=jnp.float32)


def pv(p, v):
    return lax.dot_general(
        p.astype(jnp.bfloat16), v, (((1,), (0,)), ((), ())), preferred_element_type=jnp.float32
    )


def softmax_parts(scores, values):
    peak = functools.reduce(jnp.maximum, [jnp.max(s, axis=-1, keepdims=True) for s in scores])
    total, acc = None, None
    for s, v in zip(scores, values):
        w = jnp.exp2((s - peak) * C2)
        t = jnp.sum(w, axis=-1, keepdims=True)
        a = pv(w, v)
        total = t if total is None else total + t
        acc = a if acc is None else acc + a
    return peak, total, acc


def video_kernel(meta, q, own, m2, p2, sib, fwd, tk, tv, prev, out):
    lo_p2 = meta[0] == 2
    hi_sib = meta[1] == 3
    hi_fwd = meta[1] == 4
    tiles = []
    for j in range(2):
        far_m, far_p = m2[j], p2[j]
        lo = jnp.where(lo_p2, far_p, far_m)
        hi = jnp.where(hi_fwd, fwd[j], jnp.where(hi_sib, sib[j], far_p))
        tiles.append((own[j], lo, hi))
    key_words = tk[...]
    value_words = tv[...]
    ok = lax.broadcasted_iota(jnp.int32, (1, key_words.shape[0]), 1) < meta[2]
    rows = 128
    for r in range(q.shape[0] // rows):
        qr = q[pl.ds(r * rows, rows), :]
        scores = [qk(qr, k) for k in tiles[0]]
        scores.append(jnp.where(ok, qk(qr, key_words), -jnp.inf))
        _, total, acc = softmax_parts(scores, list(tiles[1]) + [value_words])
        out[pl.ds(r * rows, rows), :] = (acc / total).astype(jnp.bfloat16)


def text_kernel(meta, q, k, v, kt, vt, peak_out, total_out, acc_out):
    h = pl.program_id(0)
    own = kt.shape[0]
    ok = lax.broadcasted_iota(jnp.int32, (1, own), 1) < meta[3]
    scores = [qk(q[...], k[...]), jnp.where(ok, qk(q[...], kt[...]), -jnp.inf)]
    peak, total, acc = softmax_parts(scores, [v[...], vt[...]])
    lane = lax.broadcasted_iota(jnp.int32, peak_out.shape, 1) == h
    peak_out[...] = jnp.where(lane, peak, jnp.where(h == 0, 0.0, peak_out[...]))
    total_out[...] = jnp.where(lane, total, jnp.where(h == 0, 1.0, total_out[...]))
    acc_out[...] = acc


def spread_heads(values, heads):
    return jnp.repeat(values[..., :heads], HD, axis=-1)


def on_device(qv, kv, vv, qt, kt, vt, key_tiles, tile_owner, text_count):
    n = lax.axis_size("ctx")
    me = lax.axis_index("ctx")
    rows, width = qv.shape
    heads = width // HD
    here = qt.shape[0]
    even = me % 2 == 0
    cols = CHUNK * HD
    chunks = heads // CHUNK

    text = lax.all_gather(jnp.stack([qt, kt, vt]), "ctx", axis=1, tiled=True)
    tq, tk, tv = text[0], text[1], text[2]

    tiles = tile_owner.shape[0]
    match = key_tiles[0][:, None] == jnp.arange(tiles, dtype=jnp.int32)[None, :]
    slots = jnp.sum(jnp.where(match, tile_owner[None, :], 0), axis=-1)
    off = slots - me
    near = jnp.where(even == (off == 1), 3, 4)
    code = jnp.where(off == 0, 0, jnp.where(off == -2, 1, jnp.where(off == 2, 2, near)))
    hi = jnp.max(code)
    lo = jnp.sum(code) - hi
    meta = jnp.stack([lo, hi, text_count[0], text_count[0] - me * here]).astype(jnp.int32)

    up = [(i, i - 2) for i in range(2, n)]
    down = [(i, i + 2) for i in range(n - 2)]
    swap = [(i, i ^ 1) for i in range(n)]
    fetched = []
    for c in range(chunks):
        sl = slice(c * cols, (c + 1) * cols)
        own = jnp.stack([kv[:, sl], vv[:, sl]])
        p2 = lax.ppermute(own, "ctx", up)
        m2 = lax.ppermute(own, "ctx", down)
        sib = lax.ppermute(own, "ctx", swap)
        fwd = lax.ppermute(jnp.where(even, p2, m2), "ctx", swap)
        fetched.append((own, m2, p2, sib, fwd))

    col = lambda h: (0, h)
    text_rows = tq.shape[0]
    smem = pl.BlockSpec(memory_space=pltpu.SMEM)
    peak, total, acc = pl.pallas_call(
        text_kernel,
        grid=(heads,),
        in_specs=[
            smem,
            pl.BlockSpec((text_rows, HD), col),
            pl.BlockSpec((rows, HD), col),
            pl.BlockSpec((rows, HD), col),
            pl.BlockSpec((here, HD), col),
            pl.BlockSpec((here, HD), col),
        ],
        out_specs=[
            pl.BlockSpec((text_rows, 128), lambda h: (0, 0)),
            pl.BlockSpec((text_rows, 128), lambda h: (0, 0)),
            pl.BlockSpec((text_rows, HD), col),
        ],
        out_shape=[
            jax.ShapeDtypeStruct((text_rows, 128), jnp.float32),
            jax.ShapeDtypeStruct((text_rows, 128), jnp.float32),
            jax.ShapeDtypeStruct((text_rows, width), jnp.float32),
        ],
        cost_estimate=pl.CostEstimate(
            flops=4 * text_rows * rows * width * 4, bytes_accessed=6 << 20, transcendentals=0
        ),
        name="text_partials",
    )(meta, tq, kv, vv, kt, vt)

    out = jnp.zeros((rows, width), jnp.bfloat16)
    for c in range(chunks):
        own, m2, p2, sib, fwd = fetched[c]
        tile_spec = pl.BlockSpec((2, rows, HD), lambda h: (0, 0, h))
        wide = lambda h, c=c: (0, h + c * CHUNK)
        out = pl.pallas_call(
            video_kernel,
            grid=(CHUNK,),
            in_specs=[smem, pl.BlockSpec((rows, HD), wide)]
            + [tile_spec] * 5
            + [pl.BlockSpec((text_rows, HD), wide)] * 2
            + [pl.BlockSpec(memory_space=pl.ANY)],
            out_specs=pl.BlockSpec((rows, HD), wide),
            out_shape=jax.ShapeDtypeStruct((rows, width), jnp.bfloat16),
            input_output_aliases={9: 0},
            compiler_params=pltpu.CompilerParams(vmem_limit_bytes=32 << 20),
            cost_estimate=pl.CostEstimate(
                flops=4 * rows * (3 * rows + text_rows) * cols * 4,
                bytes_accessed=8 << 20,
                transcendentals=0,
            ),
            name="video_chunk",
        )(meta, qv, own, m2, p2, sib, fwd, tk, tv, out)

    blocks = n
    stats = jnp.stack([peak, total]).reshape(2, blocks, here, 128)
    acc = acc.reshape(blocks, here, width)
    step = 1
    while step < n:
        blocks //= 2
        bit = (me // step) % 2
        pairs = [(i, i ^ step) for i in range(n)]
        stats4 = stats.reshape(2, blocks, 2, here, 128)
        acc4 = acc.reshape(blocks, 2, here, width)
        pick = lambda x, b, ax: jnp.where(
            b == 0, lax.index_in_dim(x, 0, ax, False), lax.index_in_dim(x, 1, ax, False)
        )
        their_s = lax.ppermute(pick(stats4, 1 - bit, 2), "ctx", pairs)
        their_a = lax.ppermute(pick(acc4, 1 - bit, 1), "ctx", pairs)
        my_s = pick(stats4, bit, 2)
        my_a = pick(acc4, bit, 1)
        joint = jnp.maximum(my_s[0], their_s[0])
        f_my = jnp.exp2((my_s[0] - joint) * C2)
        f_their = jnp.exp2((their_s[0] - joint) * C2)
        stats = jnp.stack([joint, my_s[1] * f_my + their_s[1] * f_their])
        acc = my_a * spread_heads(f_my, heads) + their_a * spread_heads(f_their, heads)
        step *= 2
    text_out = (acc[0] / spread_heads(stats[1, 0], heads)).astype(jnp.bfloat16)
    return (out, text_out)


def solution(mesh):
    split = P(("groups", "ctx"), None)
    return jax.shard_map(
        on_device,
        mesh=mesh,
        in_specs=(split,) * 7 + (P("groups"), P("groups")),
        out_specs=(split, split),
        check_vma=False,
    )
```

```python
import functools
import math

import jax
import jax.numpy as jnp
from jax import lax
from jax.experimental import pallas as pl
from jax.experimental.pallas import tpu as pltpu
from jax.sharding import PartitionSpec as P

TILE = 384
HD = 128
REACH = 2
CHUNK = 3
C2 = math.log2(math.e) / math.sqrt(HD)


def qk(q, k):
    return lax.dot_general(q, k, (((1,), (1,)), ((), ())), preferred_element_type=jnp.float32)


def pv(p, v):
    return lax.dot_general(
        p.astype(jnp.bfloat16), v, (((1,), (0,)), ((), ())), preferred_element_type=jnp.float32
    )


def softmax_parts(scores, values):
    peak = functools.reduce(jnp.maximum, [jnp.max(s, axis=-1, keepdims=True) for s in scores])
    total, acc = None, None
    for s, v in zip(scores, values):
        w = jnp.exp2((s - peak) * C2)
        t = jnp.sum(w, axis=-1, keepdims=True)
        a = pv(w, v)
        total = t if total is None else total + t
        acc = a if acc is None else acc + a
    return peak, total, acc


def video_kernel(meta, q, own, m2, p2, sib, fwd, tk, tv, prev, out):
    lo_p2 = meta[0] == 2
    hi_sib = meta[1] == 3
    hi_fwd = meta[1] == 4
    tiles = []
    for j in range(2):
        far_m, far_p = m2[j], p2[j]
        lo = jnp.where(lo_p2, far_p, far_m)
        hi = jnp.where(hi_fwd, fwd[j], jnp.where(hi_sib, sib[j], far_p))
        tiles.append((own[j], lo, hi))
    key_words = tk[...]
    value_words = tv[...]
    ok = lax.broadcasted_iota(jnp.int32, (1, key_words.shape[0]), 1) < meta[2]
    rows = 128
    for r in range(q.shape[0] // rows):
        qr = q[pl.ds(r * rows, rows), :]
        scores = [qk(qr, k) for k in tiles[0]]
        scores.append(jnp.where(ok, qk(qr, key_words), -jnp.inf))
        _, total, acc = softmax_parts(scores, list(tiles[1]) + [value_words])
        out[pl.ds(r * rows, rows), :] = (acc / total).astype(jnp.bfloat16)


def text_kernel(meta, q, k, v, kt, vt, peak_out, total_out, acc_out):
    h = pl.program_id(0)
    own = kt.shape[0]
    ok = lax.broadcasted_iota(jnp.int32, (1, own), 1) < meta[3]
    scores = [qk(q[...], k[...]), jnp.where(ok, qk(q[...], kt[...]), -jnp.inf)]
    peak, total, acc = softmax_parts(scores, [v[...], vt[...]])
    lane = lax.broadcasted_iota(jnp.int32, peak_out.shape, 1) == h
    peak_out[...] = jnp.where(lane, peak, jnp.where(h == 0, 0.0, peak_out[...]))
    total_out[...] = jnp.where(lane, total, jnp.where(h == 0, 1.0, total_out[...]))
    acc_out[...] = acc


def spread_heads(values, heads):
    return jnp.repeat(values[..., :heads], HD, axis=-1)


def on_device(qv, kv, vv, qt, kt, vt, key_tiles, tile_owner, text_count):
    n = lax.axis_size("ctx")
    me = lax.axis_index("ctx")
    rows, width = qv.shape
    heads = width // HD
    here = qt.shape[0]
    even = me % 2 == 0
    cols = CHUNK * HD
    chunks = heads // CHUNK

    text = lax.all_gather(jnp.stack([qt, kt, vt]), "ctx", axis=1, tiled=True)
    tq, tk, tv = text[0], text[1], text[2]

    tiles = tile_owner.shape[0]
    match = key_tiles[0][:, None] == jnp.arange(tiles, dtype=jnp.int32)[None, :]
    slots = jnp.sum(jnp.where(match, tile_owner[None, :], 0), axis=-1)
    off = slots - me
    near = jnp.where(even == (off == 1), 3, 4)
    code = jnp.where(off == 0, 0, jnp.where(off == -2, 1, jnp.where(off == 2, 2, near)))
    hi = jnp.max(code)
    lo = jnp.sum(code) - hi
    meta = jnp.stack([lo, hi, text_count[0], text_count[0] - me * here]).astype(jnp.int32)

    up = [(i, i - 2) for i in range(2, n)]
    down = [(i, i + 2) for i in range(n - 2)]
    swap = [(i, i ^ 1) for i in range(n)]
    fetched = []
    for c in range(chunks):
        sl = slice(c * cols, (c + 1) * cols)
        own = jnp.stack([kv[:, sl], vv[:, sl]])
        p2 = lax.ppermute(own, "ctx", up)
        m2 = lax.ppermute(own, "ctx", down)
        sib = lax.ppermute(own, "ctx", swap)
        fwd = lax.ppermute(jnp.where(even, p2, m2), "ctx", swap)
        fetched.append((own, m2, p2, sib, fwd))

    col = lambda h: (0, h)
    text_rows = tq.shape[0]
    smem = pl.BlockSpec(memory_space=pltpu.SMEM)
    peak, total, acc = pl.pallas_call(
        text_kernel,
        grid=(heads,),
        in_specs=[
            smem,
            pl.BlockSpec((text_rows, HD), col),
            pl.BlockSpec((rows, HD), col),
            pl.BlockSpec((rows, HD), col),
            pl.BlockSpec((here, HD), col),
            pl.BlockSpec((here, HD), col),
        ],
        out_specs=[
            pl.BlockSpec((text_rows, 128), lambda h: (0, 0)),
            pl.BlockSpec((text_rows, 128), lambda h: (0, 0)),
            pl.BlockSpec((text_rows, HD), col),
        ],
        out_shape=[
            jax.ShapeDtypeStruct((text_rows, 128), jnp.float32),
            jax.ShapeDtypeStruct((text_rows, 128), jnp.float32),
            jax.ShapeDtypeStruct((text_rows, width), jnp.float32),
        ],
        cost_estimate=pl.CostEstimate(
            flops=4 * text_rows * rows * width * 4, bytes_accessed=6 << 20, transcendentals=0
        ),
        name="text_partials",
    )(meta, tq, kv, vv, kt, vt)

    out = jnp.zeros((rows, width), jnp.bfloat16)
    for c in range(chunks):
        own, m2, p2, sib, fwd = fetched[c]
        tile_spec = pl.BlockSpec((2, rows, HD), lambda h: (0, 0, h))
        wide = lambda h, c=c: (0, h + c * CHUNK)
        out = pl.pallas_call(
            video_kernel,
            grid=(CHUNK,),
            in_specs=[smem, pl.BlockSpec((rows, HD), wide)]
            + [tile_spec] * 5
            + [pl.BlockSpec((text_rows, HD), wide)] * 2
            + [pl.BlockSpec(memory_space=pl.ANY)],
            out_specs=pl.BlockSpec((rows, HD), wide),
            out_shape=jax.ShapeDtypeStruct((rows, width), jnp.bfloat16),
            input_output_aliases={9: 0},
            compiler_params=pltpu.CompilerParams(vmem_limit_bytes=32 << 20),
            cost_estimate=pl.CostEstimate(
                flops=4 * rows * (3 * rows + text_rows) * cols * 4,
                bytes_accessed=8 << 20,
                transcendentals=0,
            ),
            name="video_chunk",
        )(meta, qv, own, m2, p2, sib, fwd, tk, tv, out)

    blocks = n
    stats = jnp.stack([peak, total]).reshape(2, blocks, here, 128)
    acc = acc.reshape(blocks, here, width)
    step = 1
    while step < n:
        blocks //= 2
        bit = (me // step) % 2
        pairs = [(i, i ^ step) for i in range(n)]
        stats4 = stats.reshape(2, blocks, 2, here, 128)
        acc4 = acc.reshape(blocks, 2, here, width)
        pick = lambda x, b, ax: jnp.where(
            b == 0, lax.index_in_dim(x, 0, ax, False), lax.index_in_dim(x, 1, ax, False)
        )
        their_s = lax.ppermute(pick(stats4, 1 - bit, 2), "ctx", pairs)
        their_a = lax.ppermute(pick(acc4, 1 - bit, 1), "ctx", pairs)
        my_s = pick(stats4, bit, 2)
        my_a = pick(acc4, bit, 1)
        joint = jnp.maximum(my_s[0], their_s[0])
        f_my = jnp.exp2((my_s[0] - joint) * C2)
        f_their = jnp.exp2((their_s[0] - joint) * C2)
        stats = jnp.stack([joint, my_s[1] * f_my + their_s[1] * f_their])
        acc = my_a * spread_heads(f_my, heads) + their_a * spread_heads(f_their, heads)
        step *= 2
    text_out = (acc[0] / spread_heads(stats[1, 0], heads)).astype(jnp.bfloat16)
    return (out, text_out)


def fused_kernel(
    n,
    meta,
    q_ref,
    k_ref,
    v_ref,
    qt_ref,
    kt_ref,
    vt_ref,
    bias_all,
    bias_own,
    out,
    text_out,
    tiles,
    tq,
    tkv,
    part,
    got_sib,
    got_pair,
    got_row,
    a_send,
    a_recv,
    b_send,
    b_recv,
    s_send,
    s_recv,
    f_send,
    f_recv,
    tz_send,
    tz_recv,
    ty_send,
    ty_recv,
    p_send,
    p_recv,
    pz_send,
    pz_recv,
):
    rows, width = q_ref.shape
    heads = width // HD
    here = qt_ref.shape[0]
    nz = n // 4
    me = lax.axis_index("ctx")
    core = lax.rem(me, 2)
    side = lax.rem(me // 2, 2)
    row = me // 4
    sib = me + 1 - 2 * core
    pair = me + 2 - 4 * side
    far_to = me + 4 - 8 * side
    has_to = jnp.logical_and(far_to >= 0, far_to < n)
    far_from = me - 4 + 8 * side
    has_from = jnp.logical_and(far_from >= 0, far_from < n)
    from_pair = core == side
    relay = jnp.where(from_pair, 1, 2)
    relay_ok = jnp.logical_or(from_pair, has_from)
    relay_in = jnp.logical_or(core != side, has_from)
    peers = [lax.rem(row + k, nz) * 4 + side * 2 + core for k in range(1, nz)]
    sources = [lax.rem(row + nz - k, nz) for k in range(1, nz)]
    ahead = min(3, heads)

    def col(h):
        return pl.ds(pl.multiple_of(h * HD, HD), HD)

    def remote(src, dst, send, recv, dev):
        return pltpu.make_async_remote_copy(
            src_ref=src,
            dst_ref=dst,
            send_sem=send,
            recv_sem=recv,
            device_id={"ctx": dev},
            device_id_type=pl.DeviceIdType.MESH,
        )

    def copy_a(h):
        return remote(tiles.at[0, h], tiles.at[1, h], a_send.at[h], a_recv.at[h], pair)

    def copy_b(h):
        return remote(tiles.at[1, h], tiles.at[2, h], b_send.at[h], b_recv.at[h], far_to)

    def copy_s(h):
        return remote(tiles.at[0, h], tiles.at[3, h], s_send.at[h], s_recv.at[h], sib)

    def copy_f(h):
        return remote(tiles.at[relay, h], tiles.at[4, h], f_send.at[h], f_recv.at[h], sib)

    def text_z(buf, i, k):
        spot = buf.at[core, side, row]
        return remote(spot, spot, tz_send.at[i, k], tz_recv.at[i, k], peers[k])

    def text_z_wait(buf, i, k):
        spot = buf.at[core, side, sources[k]]
        remote(spot, spot, tz_send.at[i, k], tz_recv.at[i, k], peers[k]).wait_recv()

    def text_y(buf, i, mine):
        spot = buf.at[core, side if mine else 1 - side]
        return remote(spot, spot, ty_send.at[i, 0], ty_recv.at[i, 0], pair)

    def text_s(buf, i, mine):
        spot = buf.at[core if mine else 1 - core]
        return remote(spot, spot, ty_send.at[i, 1], ty_recv.at[i, 1], sib)

    barrier = pltpu.get_barrier_semaphore()
    for peer in [sib, pair] + peers:
        pl.semaphore_signal(
            barrier, inc=1, device_id={"ctx": peer}, device_id_type=pl.DeviceIdType.MESH
        )

    tq[core, side, row] = qt_ref[...]
    tkv[core, side, row, 0] = kt_ref[...]
    tkv[core, side, row, 1] = vt_ref[...]

    def stage_own(h, _):
        tiles[0, h, 0] = k_ref[:, col(h)]
        tiles[0, h, 1] = v_ref[:, col(h)]
        return 0

    lax.fori_loop(0, heads, stage_own, 0)
    part[:, :, :, :, width:] = jnp.zeros((2, 2, nz, here, 256), jnp.float32)
    pl.semaphore_wait(barrier, nz + 1)

    for k in range(nz - 1):
        text_z(tq, 0, k).start()
    for h in range(ahead):
        copy_a(h).start()
        copy_s(h).start()
    for k in range(nz - 1):
        text_z(tkv, 1, k).start()

    def relay_step(h):
        @pl.when(has_from)
        def _():
            copy_b(h).wait_recv()

        @pl.when(relay_ok)
        def _():
            copy_f(h).start()

    def pump(t):
        copy_a(t).wait_recv()

        @pl.when(has_to)
        def _():
            copy_b(t).start()

        def more():
            copy_a(t + ahead).start()
            copy_s(t + ahead).start()

        if isinstance(t, int):
            if t + ahead < heads:
                more()
            if t > 0:
                relay_step(t - 1)
        else:
            pl.when(t + ahead < heads)(more)
            relay_step(t - 1)

    def text_head(h, _):
        q = tq[:, :, :, :, col(h)].reshape(n * here, HD)
        scores = [qk(q, tiles[0, h, 0]), qk(q, kt_ref[:, col(h)]) + bias_own[...]]
        peak, total, acc = softmax_parts(scores, [tiles[0, h, 1], vt_ref[:, col(h)]])
        part[:, :, :, :, col(h)] = acc.reshape(2, 2, nz, here, HD)
        lane = lax.broadcasted_iota(jnp.int32, (n * here, 128), 1) == h
        for base, value in ((width, peak), (width + 128, total)):
            old = part[:, :, :, :, base : base + 128].reshape(n * here, 128)
            new = jnp.where(lane, value, old)
            part[:, :, :, :, base : base + 128] = new.reshape(2, 2, nz, here, 128)
        return 0

    lo_far = meta[0] == 2
    hi_sib = meta[1] == 3
    hi_fwd = meta[1] == 4

    def video_head(h):
        copy_s(h).wait_recv()

        @pl.when(relay_in)
        def _():
            copy_f(h).wait_recv()

        picked = []
        for j in range(2):
            near, far = tiles[1, h, j], tiles[2, h, j]
            lo = jnp.where(lo_far, far, near)
            hi = jnp.where(hi_fwd, tiles[4, h, j], jnp.where(hi_sib, tiles[3, h, j], far))
            words = tkv[:, :, :, j, :, col(h)].reshape(n * here, HD)
            picked.append((tiles[0, h, j], lo, hi, words))
        block = 128
        for r in range(rows // block):
            qr = q_ref[r * block : (r + 1) * block, col(h)]
            scores = [qk(qr, key) for key in picked[0]]
            scores[3] = scores[3] + bias_all[...]
            _, total, acc = softmax_parts(scores, picked[1])
            out[r * block : (r + 1) * block, col(h)] = (acc / total).astype(jnp.bfloat16)

    def joined(first, second):
        peak1, peak2 = first[:, width : width + 128], second[:, width : width + 128]
        joint = jnp.maximum(peak1, peak2)
        f1, f2 = jnp.exp2((peak1 - joint) * C2), jnp.exp2((peak2 - joint) * C2)
        total = first[:, width + 128 :] * f1 + second[:, width + 128 :] * f2
        pieces = [
            first[:, h * HD : (h + 1) * HD] * f1[:, h : h + 1]
            + second[:, h * HD : (h + 1) * HD] * f2[:, h : h + 1]
            for h in range(heads)
        ]
        return pieces + [joint, total]

    def store_joined(view, pieces):
        for i, piece in enumerate(pieces):
            view[:, i * 128 : (i + 1) * 128] = piece

    def part_s():
        return remote(part.at[1 - core], got_sib, p_send.at[0], p_recv.at[0], sib)

    def part_y():
        return remote(part.at[core, 1 - side], got_pair, p_send.at[1], p_recv.at[1], pair)

    def part_z(k):
        there = lax.rem(row + k + 1, nz)
        return remote(
            part.at[core, side, there], got_row.at[k], pz_send.at[k], pz_recv.at[k], peers[k]
        )

    pump(0)
    for k in range(nz - 1):
        text_z_wait(tq, 0, k)
    text_y(tq, 0, True).start()
    pump(1)
    text_y(tq, 0, False).wait_recv()
    text_s(tq, 0, True).start()
    for k in range(nz - 1):
        text_z_wait(tkv, 1, k)
    text_y(tkv, 1, True).start()
    pump(2)
    text_s(tq, 0, False).wait_recv()

    batch = heads // 4

    def text_batch(i, _):
        lax.fori_loop(i * batch, (i + 1) * batch, text_head, 0)
        pump(3 + i)
        return 0

    lax.fori_loop(0, 4, text_batch, 0)
    part_s().start()
    text_y(tkv, 1, False).wait_recv()
    text_s(tkv, 1, True).start()
    pump(7)
    text_s(tkv, 1, False).wait_recv()

    def with_pump(h, _):
        pump(8 + h)
        video_head(h)
        return 0

    def only_video(h, _):
        video_head(h)
        return 0

    first = heads - 8
    lax.fori_loop(0, first, with_pump, 0)
    relay_step(heads - 1)

    part_s().wait_recv()

    def join_sib(i, _):
        y, z = i // nz, lax.rem(i, nz)
        store_joined(part.at[core, y, z], joined(part[core, y, z], got_sib[y, z]))
        return 0

    lax.fori_loop(0, 2 * nz, join_sib, 0)
    part_y().start()
    lax.fori_loop(first, first + 3, only_video, 0)
    part_y().wait_recv()

    def join_pair(z, _):
        store_joined(part.at[core, side, z], joined(part[core, side, z], got_pair[z]))
        return 0

    lax.fori_loop(0, nz, join_pair, 0)
    for k in range(nz - 1):
        part_z(k).start()
    lax.fori_loop(first + 3, heads, only_video, 0)
    whole = part[core, side, row]
    for k in range(nz - 1):
        part_z(k).wait_recv()
        whole = jnp.concatenate(joined(whole, got_row[k]), axis=1)
    for h in range(heads):
        total = whole[:, width + 128 + h : width + 129 + h]
        text_out[:, h * HD : (h + 1) * HD] = (whole[:, h * HD : (h + 1) * HD] / total).astype(
            jnp.bfloat16
        )

    for i, buf in enumerate((tq, tkv)):
        for k in range(nz - 1):
            text_z(buf, i, k).wait_send()
        text_y(buf, i, True).wait_send()
        text_s(buf, i, True).wait_send()
    part_s().wait_send()
    part_y().wait_send()
    for k in range(nz - 1):
        part_z(k).wait_send()

    def drain(h, _):
        copy_a(h).wait_send()
        copy_s(h).wait_send()

        @pl.when(has_to)
        def _():
            copy_b(h).wait_send()

        @pl.when(relay_ok)
        def _():
            copy_f(h).wait_send()

        return 0

    lax.fori_loop(0, heads, drain, 0)


def fused(qv, kv, vv, qt, kt, vt, key_tiles, tile_owner, text_count):
    n = lax.axis_size("ctx")
    me = lax.axis_index("ctx")
    rows, width = qv.shape
    heads = width // HD
    here = qt.shape[0]
    nz = n // 4
    tile_count = tile_owner.shape[0]
    match = key_tiles[0][:, None] == jnp.arange(tile_count, dtype=jnp.int32)[None, :]
    off = jnp.sum(jnp.where(match, tile_owner[None, :], 0), axis=-1) - me
    side_sign = jnp.where((me // 2) % 2 == 0, 2, -2)
    sib_sign = jnp.where(me % 2 == 0, 1, -1)
    code = jnp.where(
        off == 0,
        0,
        jnp.where(
            off == side_sign,
            1,
            jnp.where(off == -side_sign, 2, jnp.where(off == sib_sign, 3, 4)),
        ),
    )
    hi = jnp.max(code)
    meta = jnp.stack([jnp.sum(code) - hi, hi]).astype(jnp.int32)
    limit = text_count[0]
    number = jnp.arange(n).reshape(nz, 2, 2).transpose(2, 1, 0).reshape(n, 1)
    place = (number * here + jnp.arange(here)[None, :]).reshape(1, n * here)
    bias_all = jnp.where(place < limit, 0.0, -jnp.inf).astype(jnp.float32)
    own_place = me * here + jnp.arange(here)[None, :]
    bias_own = jnp.where(own_place < limit, 0.0, -jnp.inf).astype(jnp.float32)

    vmem = pl.BlockSpec(memory_space=pltpu.VMEM)
    dma = pltpu.SemaphoreType.DMA
    wide = width + 256
    return pl.pallas_call(
        functools.partial(fused_kernel, n),
        in_specs=[pl.BlockSpec(memory_space=pltpu.SMEM)] + [vmem] * 8,
        out_specs=[vmem, vmem],
        out_shape=[
            jax.ShapeDtypeStruct((rows, width), jnp.bfloat16),
            jax.ShapeDtypeStruct((here, width), jnp.bfloat16),
        ],
        scratch_shapes=[
            pltpu.VMEM((5, heads, 2, rows, HD), jnp.bfloat16),
            pltpu.VMEM((2, 2, nz, here, width), jnp.bfloat16),
            pltpu.VMEM((2, 2, nz, 2, here, width), jnp.bfloat16),
            pltpu.VMEM((2, 2, nz, here, wide), jnp.float32),
            pltpu.VMEM((2, nz, here, wide), jnp.float32),
            pltpu.VMEM((nz, here, wide), jnp.float32),
            pltpu.VMEM((nz - 1, here, wide), jnp.float32),
        ]
        + [dma((heads,))] * 8
        + [dma((2, nz - 1))] * 2
        + [dma((2, 2))] * 2
        + [dma((2,))] * 2
        + [dma((nz - 1,))] * 2,
        compiler_params=pltpu.CompilerParams(
            collective_id=0, has_side_effects=True, vmem_limit_bytes=48 << 20
        ),
        name="tile_attention",
    )(meta, qv, kv, vv, qt, kt, vt, bias_all, bias_own)


def whole_device(*args):
    n = lax.axis_size("ctx")
    rows, width = args[0].shape
    here = args[3].shape[0]
    if rows == TILE and n % 4 == 0 and n >= 8 and here % 16 == 0 and width // HD == 12:
        return fused(*args)
    return on_device(*args)


def solution(mesh):
    split = P(("groups", "ctx"), None)
    return jax.shard_map(
        whole_device,
        mesh=mesh,
        in_specs=(split,) * 7 + (P("groups"), P("groups")),
        out_specs=(split, split),
        check_vma=False,
    )
```

```python
import functools
import math

import jax
import jax.numpy as jnp
from jax import lax
from jax.experimental import pallas as pl
from jax.experimental.pallas import tpu as pltpu
from jax.sharding import PartitionSpec as P

TILE = 384
HD = 128
REACH = 2
CHUNK = 3
C2 = math.log2(math.e) / math.sqrt(HD)


def qk(q, k):
    return lax.dot_general(q, k, (((1,), (1,)), ((), ())), preferred_element_type=jnp.float32)


def pv(p, v):
    return lax.dot_general(
        p.astype(jnp.bfloat16), v, (((1,), (0,)), ((), ())), preferred_element_type=jnp.float32
    )


def softmax_parts(scores, values):
    peak = functools.reduce(jnp.maximum, [jnp.max(s, axis=-1, keepdims=True) for s in scores])
    total, acc = None, None
    for s, v in zip(scores, values):
        w = jnp.exp2((s - peak) * C2)
        t = jnp.sum(w, axis=-1, keepdims=True)
        a = pv(w, v)
        total = t if total is None else total + t
        acc = a if acc is None else acc + a
    return peak, total, acc


def video_kernel(meta, q, own, m2, p2, sib, fwd, tk, tv, prev, out):
    lo_p2 = meta[0] == 2
    hi_sib = meta[1] == 3
    hi_fwd = meta[1] == 4
    tiles = []
    for j in range(2):
        far_m, far_p = m2[j], p2[j]
        lo = jnp.where(lo_p2, far_p, far_m)
        hi = jnp.where(hi_fwd, fwd[j], jnp.where(hi_sib, sib[j], far_p))
        tiles.append((own[j], lo, hi))
    key_words = tk[...]
    value_words = tv[...]
    ok = lax.broadcasted_iota(jnp.int32, (1, key_words.shape[0]), 1) < meta[2]
    rows = 128
    for r in range(q.shape[0] // rows):
        qr = q[pl.ds(r * rows, rows), :]
        scores = [qk(qr, k) for k in tiles[0]]
        scores.append(jnp.where(ok, qk(qr, key_words), -jnp.inf))
        _, total, acc = softmax_parts(scores, list(tiles[1]) + [value_words])
        out[pl.ds(r * rows, rows), :] = (acc / total).astype(jnp.bfloat16)


def text_kernel(meta, q, k, v, kt, vt, peak_out, total_out, acc_out):
    h = pl.program_id(0)
    own = kt.shape[0]
    ok = lax.broadcasted_iota(jnp.int32, (1, own), 1) < meta[3]
    scores = [qk(q[...], k[...]), jnp.where(ok, qk(q[...], kt[...]), -jnp.inf)]
    peak, total, acc = softmax_parts(scores, [v[...], vt[...]])
    lane = lax.broadcasted_iota(jnp.int32, peak_out.shape, 1) == h
    peak_out[...] = jnp.where(lane, peak, jnp.where(h == 0, 0.0, peak_out[...]))
    total_out[...] = jnp.where(lane, total, jnp.where(h == 0, 1.0, total_out[...]))
    acc_out[...] = acc


def spread_heads(values, heads):
    return jnp.repeat(values[..., :heads], HD, axis=-1)


def on_device(qv, kv, vv, qt, kt, vt, key_tiles, tile_owner, text_count):
    n = lax.axis_size("ctx")
    me = lax.axis_index("ctx")
    rows, width = qv.shape
    heads = width // HD
    here = qt.shape[0]
    even = me % 2 == 0
    cols = CHUNK * HD
    chunks = heads // CHUNK

    text = lax.all_gather(jnp.stack([qt, kt, vt]), "ctx", axis=1, tiled=True)
    tq, tk, tv = text[0], text[1], text[2]

    tiles = tile_owner.shape[0]
    match = key_tiles[0][:, None] == jnp.arange(tiles, dtype=jnp.int32)[None, :]
    slots = jnp.sum(jnp.where(match, tile_owner[None, :], 0), axis=-1)
    off = slots - me
    near = jnp.where(even == (off == 1), 3, 4)
    code = jnp.where(off == 0, 0, jnp.where(off == -2, 1, jnp.where(off == 2, 2, near)))
    hi = jnp.max(code)
    lo = jnp.sum(code) - hi
    meta = jnp.stack([lo, hi, text_count[0], text_count[0] - me * here]).astype(jnp.int32)

    up = [(i, i - 2) for i in range(2, n)]
    down = [(i, i + 2) for i in range(n - 2)]
    swap = [(i, i ^ 1) for i in range(n)]
    fetched = []
    for c in range(chunks):
        sl = slice(c * cols, (c + 1) * cols)
        own = jnp.stack([kv[:, sl], vv[:, sl]])
        p2 = lax.ppermute(own, "ctx", up)
        m2 = lax.ppermute(own, "ctx", down)
        sib = lax.ppermute(own, "ctx", swap)
        fwd = lax.ppermute(jnp.where(even, p2, m2), "ctx", swap)
        fetched.append((own, m2, p2, sib, fwd))

    col = lambda h: (0, h)
    text_rows = tq.shape[0]
    smem = pl.BlockSpec(memory_space=pltpu.SMEM)
    peak, total, acc = pl.pallas_call(
        text_kernel,
        grid=(heads,),
        in_specs=[
            smem,
            pl.BlockSpec((text_rows, HD), col),
            pl.BlockSpec((rows, HD), col),
            pl.BlockSpec((rows, HD), col),
            pl.BlockSpec((here, HD), col),
            pl.BlockSpec((here, HD), col),
        ],
        out_specs=[
            pl.BlockSpec((text_rows, 128), lambda h: (0, 0)),
            pl.BlockSpec((text_rows, 128), lambda h: (0, 0)),
            pl.BlockSpec((text_rows, HD), col),
        ],
        out_shape=[
            jax.ShapeDtypeStruct((text_rows, 128), jnp.float32),
            jax.ShapeDtypeStruct((text_rows, 128), jnp.float32),
            jax.ShapeDtypeStruct((text_rows, width), jnp.float32),
        ],
        cost_estimate=pl.CostEstimate(
            flops=4 * text_rows * rows * width * 4, bytes_accessed=6 << 20, transcendentals=0
        ),
        name="text_partials",
    )(meta, tq, kv, vv, kt, vt)

    out = jnp.zeros((rows, width), jnp.bfloat16)
    for c in range(chunks):
        own, m2, p2, sib, fwd = fetched[c]
        tile_spec = pl.BlockSpec((2, rows, HD), lambda h: (0, 0, h))
        wide = lambda h, c=c: (0, h + c * CHUNK)
        out = pl.pallas_call(
            video_kernel,
            grid=(CHUNK,),
            in_specs=[smem, pl.BlockSpec((rows, HD), wide)]
            + [tile_spec] * 5
            + [pl.BlockSpec((text_rows, HD), wide)] * 2
            + [pl.BlockSpec(memory_space=pl.ANY)],
            out_specs=pl.BlockSpec((rows, HD), wide),
            out_shape=jax.ShapeDtypeStruct((rows, width), jnp.bfloat16),
            input_output_aliases={9: 0},
            compiler_params=pltpu.CompilerParams(vmem_limit_bytes=32 << 20),
            cost_estimate=pl.CostEstimate(
                flops=4 * rows * (3 * rows + text_rows) * cols * 4,
                bytes_accessed=8 << 20,
                transcendentals=0,
            ),
            name="video_chunk",
        )(meta, qv, own, m2, p2, sib, fwd, tk, tv, out)

    blocks = n
    stats = jnp.stack([peak, total]).reshape(2, blocks, here, 128)
    acc = acc.reshape(blocks, here, width)
    step = 1
    while step < n:
        blocks //= 2
        bit = (me // step) % 2
        pairs = [(i, i ^ step) for i in range(n)]
        stats4 = stats.reshape(2, blocks, 2, here, 128)
        acc4 = acc.reshape(blocks, 2, here, width)
        pick = lambda x, b, ax: jnp.where(
            b == 0, lax.index_in_dim(x, 0, ax, False), lax.index_in_dim(x, 1, ax, False)
        )
        their_s = lax.ppermute(pick(stats4, 1 - bit, 2), "ctx", pairs)
        their_a = lax.ppermute(pick(acc4, 1 - bit, 1), "ctx", pairs)
        my_s = pick(stats4, bit, 2)
        my_a = pick(acc4, bit, 1)
        joint = jnp.maximum(my_s[0], their_s[0])
        f_my = jnp.exp2((my_s[0] - joint) * C2)
        f_their = jnp.exp2((their_s[0] - joint) * C2)
        stats = jnp.stack([joint, my_s[1] * f_my + their_s[1] * f_their])
        acc = my_a * spread_heads(f_my, heads) + their_a * spread_heads(f_their, heads)
        step *= 2
    text_out = (acc[0] / spread_heads(stats[1, 0], heads)).astype(jnp.bfloat16)
    return (out, text_out)


def fused_kernel(
    n,
    listed,
    owner,
    count,
    q_hbm,
    k_hbm,
    v_hbm,
    qt_hbm,
    kt_hbm,
    vt_hbm,
    out,
    text_out,
    q_ref,
    tiles,
    tq,
    tkv,
    part,
    got_sib,
    got_pair,
    got_row,
    a_send,
    a_recv,
    b_send,
    b_recv,
    s_send,
    s_recv,
    f_send,
    f_recv,
    tz_send,
    tz_recv,
    ty_send,
    ty_recv,
    p_send,
    p_recv,
    pz_send,
    pz_recv,
    own_sem,
    in_sem,
):
    rows, width = q_ref.shape
    heads = width // HD
    here = qt_hbm.shape[0]
    nz = n // 4
    me = lax.axis_index("ctx")
    core = lax.rem(me, 2)
    side = lax.rem(me // 2, 2)
    row = me // 4
    sib = me + 1 - 2 * core
    pair = me + 2 - 4 * side
    far_to = me + 4 - 8 * side
    has_to = jnp.logical_and(far_to >= 0, far_to < n)
    far_from = me - 4 + 8 * side
    has_from = jnp.logical_and(far_from >= 0, far_from < n)
    from_pair = core == side
    relay = jnp.where(from_pair, 1, 2)
    relay_ok = jnp.logical_or(from_pair, has_from)
    relay_in = jnp.logical_or(core != side, has_from)
    peers = [lax.rem(row + k, nz) * 4 + side * 2 + core for k in range(1, nz)]
    sources = [lax.rem(row + nz - k, nz) for k in range(1, nz)]
    ahead = min(3, heads)

    def col(h):
        return pl.ds(pl.multiple_of(h * HD, HD), HD)

    def remote(src, dst, send, recv, dev):
        return pltpu.make_async_remote_copy(
            src_ref=src,
            dst_ref=dst,
            send_sem=send,
            recv_sem=recv,
            device_id={"ctx": dev},
            device_id_type=pl.DeviceIdType.MESH,
        )

    def copy_a(h):
        return remote(tiles.at[0, h], tiles.at[1, h], a_send.at[h], a_recv.at[h], pair)

    def copy_b(h):
        return remote(tiles.at[1, h], tiles.at[2, h], b_send.at[h], b_recv.at[h], far_to)

    def copy_s(h):
        return remote(tiles.at[0, h], tiles.at[3, h], s_send.at[h], s_recv.at[h], sib)

    def copy_f(h):
        return remote(tiles.at[relay, h], tiles.at[4, h], f_send.at[h], f_recv.at[h], sib)

    def text_z(buf, i, k):
        spot = buf.at[core, side, row]
        return remote(spot, spot, tz_send.at[i, k], tz_recv.at[i, k], peers[k])

    def text_z_wait(buf, i, k):
        spot = buf.at[core, side, sources[k]]
        remote(spot, spot, tz_send.at[i, k], tz_recv.at[i, k], peers[k]).wait_recv()

    def text_y(buf, i, mine):
        spot = buf.at[core, side if mine else 1 - side]
        return remote(spot, spot, ty_send.at[i, 0], ty_recv.at[i, 0], pair)

    def text_s(buf, i, mine):
        spot = buf.at[core if mine else 1 - core]
        return remote(spot, spot, ty_send.at[i, 1], ty_recv.at[i, 1], sib)

    barrier = pltpu.get_barrier_semaphore()
    for peer in [sib, pair] + peers:
        pl.semaphore_signal(
            barrier, inc=1, device_id={"ctx": peer}, device_id_type=pl.DeviceIdType.MESH
        )

    def own_copy(h, j):
        return pltpu.make_async_copy(
            (k_hbm, v_hbm)[j].at[:, col(h)], tiles.at[0, h, j], own_sem.at[j, h]
        )

    text_in = [
        pltpu.make_async_copy(qt_hbm, tq.at[core, side, row], in_sem.at[0]),
        pltpu.make_async_copy(kt_hbm, tkv.at[core, side, row, 0], in_sem.at[1]),
        pltpu.make_async_copy(vt_hbm, tkv.at[core, side, row, 1], in_sem.at[2]),
    ]
    query_in = pltpu.make_async_copy(q_hbm, q_ref, in_sem.at[3])
    for copy in text_in:
        copy.start()

    def own_start(h, _):
        own_copy(h, 0).start()
        own_copy(h, 1).start()
        return 0

    def own_wait(h, _):
        own_copy(h, 0).wait()
        own_copy(h, 1).wait()
        return 0

    lax.fori_loop(0, heads, own_start, 0)
    query_in.start()
    part[:, :, :, :, width:] = jnp.zeros((2, 2, nz, here, 256), jnp.float32)

    limit = count[0]
    spot = lax.broadcasted_iota(jnp.int32, (1, n * here), 1)
    lane_r = spot & (here - 1)
    lane_z = (spot >> (here.bit_length() - 1)) & (nz - 1)
    lane_y = (spot >> ((here * nz).bit_length() - 1)) & 1
    lane_c = spot >> ((here * nz * 2).bit_length() - 1)
    place = (lane_z * 4 + lane_y * 2 + lane_c) * here + lane_r
    bias_all = jnp.where(place < limit, 0.0, -jnp.inf).astype(jnp.float32)
    own_place = me * here + lax.broadcasted_iota(jnp.int32, (1, here), 1)
    bias_own = jnp.where(own_place < limit, 0.0, -jnp.inf).astype(jnp.float32)

    for copy in text_in:
        copy.wait()
    pl.semaphore_wait(barrier, nz + 1)

    for k in range(nz - 1):
        text_z(tq, 0, k).start()
    lax.fori_loop(0, ahead, own_wait, 0)
    for h in range(ahead):
        copy_a(h).start()
        copy_s(h).start()
    for k in range(nz - 1):
        text_z(tkv, 1, k).start()
    lax.fori_loop(ahead, heads, own_wait, 0)

    def relay_step(h):
        @pl.when(has_from)
        def _():
            copy_b(h).wait_recv()

        @pl.when(relay_ok)
        def _():
            copy_f(h).start()

    def pump(t):
        copy_a(t).wait_recv()

        @pl.when(has_to)
        def _():
            copy_b(t).start()

        def more():
            copy_a(t + ahead).start()
            copy_s(t + ahead).start()

        if isinstance(t, int):
            if t + ahead < heads:
                more()
            if t > 0:
                relay_step(t - 1)
        else:
            pl.when(t + ahead < heads)(more)
            relay_step(t - 1)

    def text_head(h, _):
        q = tq[:, :, :, :, col(h)].reshape(n * here, HD)
        scores = [qk(q, tiles[0, h, 0]), qk(q, tkv[core, side, row, 0, :, col(h)]) + bias_own]
        peak, total, acc = softmax_parts(scores, [tiles[0, h, 1], tkv[core, side, row, 1, :, col(h)]])
        part[:, :, :, :, col(h)] = acc.reshape(2, 2, nz, here, HD)
        lane = lax.broadcasted_iota(jnp.int32, (n * here, 128), 1) == h
        for base, value in ((width, peak), (width + 128, total)):
            old = part[:, :, :, :, base : base + 128].reshape(n * here, 128)
            new = jnp.where(lane, value, old)
            part[:, :, :, :, base : base + 128] = new.reshape(2, 2, nz, here, 128)
        return 0

    codes = []
    for j in range(listed.shape[1]):
        off = owner[listed[0, j]] - me
        code = jnp.where(off == sib - me, 3, 4)
        code = jnp.where(off == me - pair, 2, code)
        code = jnp.where(off == pair - me, 1, code)
        codes.append(jnp.where(off == 0, 0, code))
    hi_code = functools.reduce(jnp.maximum, codes)
    lo_code = sum(codes) - hi_code
    lo_far = lo_code == 2
    hi_sib = hi_code == 3
    hi_fwd = hi_code == 4

    def video_head(h):
        copy_s(h).wait_recv()

        @pl.when(relay_in)
        def _():
            copy_f(h).wait_recv()

        picked = []
        for j in range(2):
            near, far = tiles[1, h, j], tiles[2, h, j]
            lo = jnp.where(lo_far, far, near)
            hi = jnp.where(hi_fwd, tiles[4, h, j], jnp.where(hi_sib, tiles[3, h, j], far))
            words = tkv[:, :, :, j, :, col(h)].reshape(n * here, HD)
            picked.append((tiles[0, h, j], lo, hi, words))
        block = 128
        for r in range(rows // block):
            qr = q_ref[r * block : (r + 1) * block, col(h)]
            scores = [qk(qr, key) for key in picked[0]]
            scores[3] = scores[3] + bias_all
            _, total, acc = softmax_parts(scores, picked[1])
            out[r * block : (r + 1) * block, col(h)] = (acc / total).astype(jnp.bfloat16)

    def joined(first, second):
        peak1, peak2 = first[:, width : width + 128], second[:, width : width + 128]
        joint = jnp.maximum(peak1, peak2)
        f1, f2 = jnp.exp2((peak1 - joint) * C2), jnp.exp2((peak2 - joint) * C2)
        total = first[:, width + 128 :] * f1 + second[:, width + 128 :] * f2
        pieces = [
            first[:, h * HD : (h + 1) * HD] * f1[:, h : h + 1]
            + second[:, h * HD : (h + 1) * HD] * f2[:, h : h + 1]
            for h in range(heads)
        ]
        return pieces + [joint, total]

    def store_joined(view, pieces):
        for i, piece in enumerate(pieces):
            view[:, i * 128 : (i + 1) * 128] = piece

    def part_s():
        return remote(part.at[1 - core], got_sib, p_send.at[0], p_recv.at[0], sib)

    def part_y():
        return remote(part.at[core, 1 - side], got_pair, p_send.at[1], p_recv.at[1], pair)

    def part_z(k):
        there = lax.rem(row + k + 1, nz)
        return remote(
            part.at[core, side, there], got_row.at[k], pz_send.at[k], pz_recv.at[k], peers[k]
        )

    def join_sib(i, _):
        y, z = i // nz, lax.rem(i, nz)
        store_joined(part.at[core, y, z], joined(part[core, y, z], got_sib[y, z]))
        return 0

    def join_pair(z, _):
        store_joined(part.at[core, side, z], joined(part[core, side, z], got_pair[z]))
        return 0

    for k in range(nz - 1):
        text_z_wait(tq, 0, k)
    text_y(tq, 0, True).start()
    pump(0)
    text_y(tq, 0, False).wait_recv()
    text_s(tq, 0, True).start()
    for k in range(nz - 1):
        text_z_wait(tkv, 1, k)
    text_y(tkv, 1, True).start()
    pump(1)
    text_s(tq, 0, False).wait_recv()
    half = heads // 2
    lax.fori_loop(0, half, text_head, 0)
    pump(2)
    lax.fori_loop(half, heads, text_head, 0)
    part_s().start()
    pump(3)
    text_y(tkv, 1, False).wait_recv()
    text_s(tkv, 1, True).start()
    part_s().wait_recv()
    lax.fori_loop(0, 2 * nz, join_sib, 0)
    part_y().start()
    pump(4)
    text_s(tkv, 1, False).wait_recv()
    query_in.wait()

    def video_pair(i, _):
        pump(5 + i)
        lax.fori_loop(2 * i, 2 * i + 2, lambda h, c: (video_head(h), c)[1], 0)
        return 0

    lax.fori_loop(0, 3, video_pair, 0)
    part_y().wait_recv()
    lax.fori_loop(0, nz, join_pair, 0)
    for k in range(nz - 1):
        part_z(k).start()

    def video_last(i, _):
        pump(8 + i)
        video_head(6 + i)
        return 0

    lax.fori_loop(0, heads - 8, video_last, 0)
    video_head(heads - 2)
    relay_step(heads - 1)
    whole = part[core, side, row]
    for k in range(nz - 1):
        part_z(k).wait_recv()
        whole = jnp.concatenate(joined(whole, got_row[k]), axis=1)
    for h in range(heads):
        total = whole[:, width + 128 + h : width + 129 + h]
        text_out[:, h * HD : (h + 1) * HD] = (whole[:, h * HD : (h + 1) * HD] / total).astype(
            jnp.bfloat16
        )
    video_head(heads - 1)

    for i, buf in enumerate((tq, tkv)):
        for k in range(nz - 1):
            text_z(buf, i, k).wait_send()
        text_y(buf, i, True).wait_send()
        text_s(buf, i, True).wait_send()
    part_s().wait_send()
    part_y().wait_send()
    for k in range(nz - 1):
        part_z(k).wait_send()

    def drain(h, _):
        copy_a(h).wait_send()
        copy_s(h).wait_send()

        @pl.when(has_to)
        def _():
            copy_b(h).wait_send()

        @pl.when(relay_ok)
        def _():
            copy_f(h).wait_send()

        return 0

    lax.fori_loop(0, heads, drain, 0)


def fused(qv, kv, vv, qt, kt, vt, key_tiles, tile_owner, text_count):
    n = lax.axis_size("ctx")
    rows, width = qv.shape
    heads = width // HD
    here = qt.shape[0]
    nz = n // 4
    vmem = pl.BlockSpec(memory_space=pltpu.VMEM)
    dma = pltpu.SemaphoreType.DMA
    wide = width + 256
    return pl.pallas_call(
        functools.partial(fused_kernel, n),
        in_specs=[pl.BlockSpec(memory_space=pltpu.SMEM)] * 3
        + [pl.BlockSpec(memory_space=pl.ANY)] * 6,
        out_specs=[vmem, vmem],
        out_shape=[
            jax.ShapeDtypeStruct((rows, width), jnp.bfloat16),
            jax.ShapeDtypeStruct((here, width), jnp.bfloat16),
        ],
        scratch_shapes=[
            pltpu.VMEM((rows, width), jnp.bfloat16),
            pltpu.VMEM((5, heads, 2, rows, HD), jnp.bfloat16),
            pltpu.VMEM((2, 2, nz, here, width), jnp.bfloat16),
            pltpu.VMEM((2, 2, nz, 2, here, width), jnp.bfloat16),
            pltpu.VMEM((2, 2, nz, here, wide), jnp.float32),
            pltpu.VMEM((2, nz, here, wide), jnp.float32),
            pltpu.VMEM((nz, here, wide), jnp.float32),
            pltpu.VMEM((nz - 1, here, wide), jnp.float32),
        ]
        + [dma((heads,))] * 8
        + [dma((2, nz - 1))] * 2
        + [dma((2, 2))] * 2
        + [dma((2,))] * 2
        + [dma((nz - 1,))] * 2
        + [dma((2, heads)), dma((4,))],
        compiler_params=pltpu.CompilerParams(
            collective_id=0, has_side_effects=True, vmem_limit_bytes=56 << 20
        ),
        name="tile_attention",
    )(key_tiles, tile_owner, text_count, qv, kv, vv, qt, kt, vt)


def whole_device(*args):
    n = lax.axis_size("ctx")
    rows, width = args[0].shape
    here = args[3].shape[0]
    if rows == TILE and n % 4 == 0 and n >= 8 and n & (n - 1) == 0 and here in (16, 32, 64) and width // HD == 12:
        return fused(*args)
    return on_device(*args)


def solution(mesh):
    split = P(("groups", "ctx"), None)
    return jax.shard_map(
        whole_device,
        mesh=mesh,
        in_specs=(split,) * 7 + (P("groups"), P("groups")),
        out_specs=(split, split),
        check_vma=False,
    )
```

```python
import functools
import math

import jax
import jax.numpy as jnp
from jax import lax
from jax.experimental import pallas as pl
from jax.experimental.pallas import tpu as pltpu
from jax.sharding import PartitionSpec as P

TILE = 384
HD = 128
REACH = 2
CHUNK = 3
C2 = math.log2(math.e) / math.sqrt(HD)


def qk(q, k):
    return lax.dot_general(q, k, (((1,), (1,)), ((), ())), preferred_element_type=jnp.float32)


def pv(p, v):
    return lax.dot_general(
        p.astype(jnp.bfloat16), v, (((1,), (0,)), ((), ())), preferred_element_type=jnp.float32
    )


def softmax_parts(scores, values):
    peak = functools.reduce(jnp.maximum, [jnp.max(s, axis=-1, keepdims=True) for s in scores])
    total, acc = None, None
    for s, v in zip(scores, values):
        w = jnp.exp2((s - peak) * C2)
        t = jnp.sum(w, axis=-1, keepdims=True)
        a = pv(w, v)
        total = t if total is None else total + t
        acc = a if acc is None else acc + a
    return peak, total, acc


def video_kernel(meta, q, own, m2, p2, sib, fwd, tk, tv, prev, out):
    lo_p2 = meta[0] == 2
    hi_sib = meta[1] == 3
    hi_fwd = meta[1] == 4
    tiles = []
    for j in range(2):
        far_m, far_p = m2[j], p2[j]
        lo = jnp.where(lo_p2, far_p, far_m)
        hi = jnp.where(hi_fwd, fwd[j], jnp.where(hi_sib, sib[j], far_p))
        tiles.append((own[j], lo, hi))
    key_words = tk[...]
    value_words = tv[...]
    ok = lax.broadcasted_iota(jnp.int32, (1, key_words.shape[0]), 1) < meta[2]
    rows = 128
    for r in range(q.shape[0] // rows):
        qr = q[pl.ds(r * rows, rows), :]
        scores = [qk(qr, k) for k in tiles[0]]
        scores.append(jnp.where(ok, qk(qr, key_words), -jnp.inf))
        _, total, acc = softmax_parts(scores, list(tiles[1]) + [value_words])
        out[pl.ds(r * rows, rows), :] = (acc / total).astype(jnp.bfloat16)


def text_kernel(meta, q, k, v, kt, vt, peak_out, total_out, acc_out):
    h = pl.program_id(0)
    own = kt.shape[0]
    ok = lax.broadcasted_iota(jnp.int32, (1, own), 1) < meta[3]
    scores = [qk(q[...], k[...]), jnp.where(ok, qk(q[...], kt[...]), -jnp.inf)]
    peak, total, acc = softmax_parts(scores, [v[...], vt[...]])
    lane = lax.broadcasted_iota(jnp.int32, peak_out.shape, 1) == h
    peak_out[...] = jnp.where(lane, peak, jnp.where(h == 0, 0.0, peak_out[...]))
    total_out[...] = jnp.where(lane, total, jnp.where(h == 0, 1.0, total_out[...]))
    acc_out[...] = acc


def spread_heads(values, heads):
    return jnp.repeat(values[..., :heads], HD, axis=-1)


def on_device(qv, kv, vv, qt, kt, vt, key_tiles, tile_owner, text_count):
    n = lax.axis_size("ctx")
    me = lax.axis_index("ctx")
    rows, width = qv.shape
    heads = width // HD
    here = qt.shape[0]
    even = me % 2 == 0
    cols = CHUNK * HD
    chunks = heads // CHUNK

    text = lax.all_gather(jnp.stack([qt, kt, vt]), "ctx", axis=1, tiled=True)
    tq, tk, tv = text[0], text[1], text[2]

    tiles = tile_owner.shape[0]
    match = key_tiles[0][:, None] == jnp.arange(tiles, dtype=jnp.int32)[None, :]
    slots = jnp.sum(jnp.where(match, tile_owner[None, :], 0), axis=-1)
    off = slots - me
    near = jnp.where(even == (off == 1), 3, 4)
    code = jnp.where(off == 0, 0, jnp.where(off == -2, 1, jnp.where(off == 2, 2, near)))
    hi = jnp.max(code)
    lo = jnp.sum(code) - hi
    meta = jnp.stack([lo, hi, text_count[0], text_count[0] - me * here]).astype(jnp.int32)

    up = [(i, i - 2) for i in range(2, n)]
    down = [(i, i + 2) for i in range(n - 2)]
    swap = [(i, i ^ 1) for i in range(n)]
    fetched = []
    for c in range(chunks):
        sl = slice(c * cols, (c + 1) * cols)
        own = jnp.stack([kv[:, sl], vv[:, sl]])
        p2 = lax.ppermute(own, "ctx", up)
        m2 = lax.ppermute(own, "ctx", down)
        sib = lax.ppermute(own, "ctx", swap)
        fwd = lax.ppermute(jnp.where(even, p2, m2), "ctx", swap)
        fetched.append((own, m2, p2, sib, fwd))

    col = lambda h: (0, h)
    text_rows = tq.shape[0]
    smem = pl.BlockSpec(memory_space=pltpu.SMEM)
    peak, total, acc = pl.pallas_call(
        text_kernel,
        grid=(heads,),
        in_specs=[
            smem,
            pl.BlockSpec((text_rows, HD), col),
            pl.BlockSpec((rows, HD), col),
            pl.BlockSpec((rows, HD), col),
            pl.BlockSpec((here, HD), col),
            pl.BlockSpec((here, HD), col),
        ],
        out_specs=[
            pl.BlockSpec((text_rows, 128), lambda h: (0, 0)),
            pl.BlockSpec((text_rows, 128), lambda h: (0, 0)),
            pl.BlockSpec((text_rows, HD), col),
        ],
        out_shape=[
            jax.ShapeDtypeStruct((text_rows, 128), jnp.float32),
            jax.ShapeDtypeStruct((text_rows, 128), jnp.float32),
            jax.ShapeDtypeStruct((text_rows, width), jnp.float32),
        ],
        cost_estimate=pl.CostEstimate(
            flops=4 * text_rows * rows * width * 4, bytes_accessed=6 << 20, transcendentals=0
        ),
        name="text_partials",
    )(meta, tq, kv, vv, kt, vt)

    out = jnp.zeros((rows, width), jnp.bfloat16)
    for c in range(chunks):
        own, m2, p2, sib, fwd = fetched[c]
        tile_spec = pl.BlockSpec((2, rows, HD), lambda h: (0, 0, h))
        wide = lambda h, c=c: (0, h + c * CHUNK)
        out = pl.pallas_call(
            video_kernel,
            grid=(CHUNK,),
            in_specs=[smem, pl.BlockSpec((rows, HD), wide)]
            + [tile_spec] * 5
            + [pl.BlockSpec((text_rows, HD), wide)] * 2
            + [pl.BlockSpec(memory_space=pl.ANY)],
            out_specs=pl.BlockSpec((rows, HD), wide),
            out_shape=jax.ShapeDtypeStruct((rows, width), jnp.bfloat16),
            input_output_aliases={9: 0},
            compiler_params=pltpu.CompilerParams(vmem_limit_bytes=32 << 20),
            cost_estimate=pl.CostEstimate(
                flops=4 * rows * (3 * rows + text_rows) * cols * 4,
                bytes_accessed=8 << 20,
                transcendentals=0,
            ),
            name="video_chunk",
        )(meta, qv, own, m2, p2, sib, fwd, tk, tv, out)

    blocks = n
    stats = jnp.stack([peak, total]).reshape(2, blocks, here, 128)
    acc = acc.reshape(blocks, here, width)
    step = 1
    while step < n:
        blocks //= 2
        bit = (me // step) % 2
        pairs = [(i, i ^ step) for i in range(n)]
        stats4 = stats.reshape(2, blocks, 2, here, 128)
        acc4 = acc.reshape(blocks, 2, here, width)
        pick = lambda x, b, ax: jnp.where(
            b == 0, lax.index_in_dim(x, 0, ax, False), lax.index_in_dim(x, 1, ax, False)
        )
        their_s = lax.ppermute(pick(stats4, 1 - bit, 2), "ctx", pairs)
        their_a = lax.ppermute(pick(acc4, 1 - bit, 1), "ctx", pairs)
        my_s = pick(stats4, bit, 2)
        my_a = pick(acc4, bit, 1)
        joint = jnp.maximum(my_s[0], their_s[0])
        f_my = jnp.exp2((my_s[0] - joint) * C2)
        f_their = jnp.exp2((their_s[0] - joint) * C2)
        stats = jnp.stack([joint, my_s[1] * f_my + their_s[1] * f_their])
        acc = my_a * spread_heads(f_my, heads) + their_a * spread_heads(f_their, heads)
        step *= 2
    text_out = (acc[0] / spread_heads(stats[1, 0], heads)).astype(jnp.bfloat16)
    return (out, text_out)


def fused_kernel(
    n,
    listed,
    owner,
    count,
    q_hbm,
    k_hbm,
    v_hbm,
    qt_hbm,
    kt_hbm,
    vt_hbm,
    out,
    text_out,
    q_ref,
    tiles,
    tq,
    tkv,
    part,
    got_sib,
    got_pair,
    pair_stats,
    sent_pair,
    got_row,
    a_send,
    a_recv,
    b_send,
    b_recv,
    s_send,
    s_recv,
    f_send,
    f_recv,
    tz_send,
    tz_recv,
    ty_send,
    ty_recv,
    p_send,
    p_recv,
    pz_send,
    pz_recv,
    own_sem,
    in_sem,
):
    rows, width = q_ref.shape
    heads = width // HD
    here = qt_hbm.shape[0]
    nz = n // 4
    me = lax.axis_index("ctx")
    core = lax.rem(me, 2)
    side = lax.rem(me // 2, 2)
    row = me // 4
    sib = me + 1 - 2 * core
    pair = me + 2 - 4 * side
    far_to = me + 4 - 8 * side
    has_to = jnp.logical_and(far_to >= 0, far_to < n)
    far_from = me - 4 + 8 * side
    has_from = jnp.logical_and(far_from >= 0, far_from < n)
    from_pair = core == side
    relay = jnp.where(from_pair, 1, 2)
    relay_ok = jnp.logical_or(from_pair, has_from)
    relay_in = jnp.logical_or(core != side, has_from)
    peers = [lax.rem(row + k, nz) * 4 + side * 2 + core for k in range(1, nz)]
    sources = [lax.rem(row + nz - k, nz) for k in range(1, nz)]
    ahead = min(3, heads)

    def col(h):
        return pl.ds(pl.multiple_of(h * HD, HD), HD)

    def remote(src, dst, send, recv, dev):
        return pltpu.make_async_remote_copy(
            src_ref=src,
            dst_ref=dst,
            send_sem=send,
            recv_sem=recv,
            device_id={"ctx": dev},
            device_id_type=pl.DeviceIdType.MESH,
        )

    def copy_a(h):
        return remote(tiles.at[0, h], tiles.at[1, h], a_send.at[h], a_recv.at[h], pair)

    def copy_b(h):
        return remote(tiles.at[1, h], tiles.at[2, h], b_send.at[h], b_recv.at[h], far_to)

    def copy_s(h):
        return remote(tiles.at[0, h], tiles.at[3, h], s_send.at[h], s_recv.at[h], sib)

    def copy_f(h):
        return remote(tiles.at[relay, h], tiles.at[4, h], f_send.at[h], f_recv.at[h], sib)

    def text_z(buf, i, k):
        spot = buf.at[core, side, row]
        return remote(spot, spot, tz_send.at[i, k], tz_recv.at[i, k], peers[k])

    def text_z_wait(buf, i, k):
        spot = buf.at[core, side, sources[k]]
        remote(spot, spot, tz_send.at[i, k], tz_recv.at[i, k], peers[k]).wait_recv()

    def text_y(buf, i, mine):
        spot = buf.at[core, side if mine else 1 - side]
        return remote(spot, spot, ty_send.at[i, 0], ty_recv.at[i, 0], pair)

    def text_s(buf, i, mine):
        spot = buf.at[core if mine else 1 - core]
        return remote(spot, spot, ty_send.at[i, 1], ty_recv.at[i, 1], sib)

    barrier = pltpu.get_barrier_semaphore()
    for peer in [sib, pair] + peers:
        pl.semaphore_signal(
            barrier, inc=1, device_id={"ctx": peer}, device_id_type=pl.DeviceIdType.MESH
        )

    def own_copy(h, j):
        return pltpu.make_async_copy(
            (k_hbm, v_hbm)[j].at[:, col(h)], tiles.at[0, h, j], own_sem.at[j, h]
        )

    text_in = [
        pltpu.make_async_copy(qt_hbm, tq.at[core, side, row], in_sem.at[0]),
        pltpu.make_async_copy(kt_hbm, tkv.at[core, side, row, 0], in_sem.at[1]),
        pltpu.make_async_copy(vt_hbm, tkv.at[core, side, row, 1], in_sem.at[2]),
    ]
    query_in = pltpu.make_async_copy(q_hbm, q_ref, in_sem.at[3])
    for copy in text_in:
        copy.start()

    def own_start(h, _):
        own_copy(h, 0).start()
        own_copy(h, 1).start()
        return 0

    def own_wait(h, _):
        own_copy(h, 0).wait()
        own_copy(h, 1).wait()
        return 0

    lax.fori_loop(0, heads, own_start, 0)
    query_in.start()
    part[:, :, :, :, width:] = jnp.zeros((2, 2, nz, here, 256), jnp.float32)

    limit = count[0]
    spot = lax.broadcasted_iota(jnp.int32, (1, n * here), 1)
    lane_r = spot & (here - 1)
    lane_z = (spot >> (here.bit_length() - 1)) & (nz - 1)
    lane_y = (spot >> ((here * nz).bit_length() - 1)) & 1
    lane_c = spot >> ((here * nz * 2).bit_length() - 1)
    place = (lane_z * 4 + lane_y * 2 + lane_c) * here + lane_r
    bias_all = jnp.where(place < limit, 0.0, -jnp.inf).astype(jnp.float32)
    own_place = me * here + lax.broadcasted_iota(jnp.int32, (1, here), 1)
    bias_own = jnp.where(own_place < limit, 0.0, -jnp.inf).astype(jnp.float32)

    for copy in text_in:
        copy.wait()
    pl.semaphore_wait(barrier, nz + 1)

    for k in range(nz - 1):
        text_z(tq, 0, k).start()
    lax.fori_loop(0, ahead, own_wait, 0)
    for h in range(ahead):
        copy_a(h).start()
        copy_s(h).start()
    for k in range(nz - 1):
        text_z(tkv, 1, k).start()
    lax.fori_loop(ahead, heads, own_wait, 0)

    def relay_step(h):
        @pl.when(has_from)
        def _():
            copy_b(h).wait_recv()

        @pl.when(relay_ok)
        def _():
            copy_f(h).start()

    def pump(t):
        copy_a(t).wait_recv()

        @pl.when(has_to)
        def _():
            copy_b(t).start()

        def more():
            copy_a(t + ahead).start()
            copy_s(t + ahead).start()

        if isinstance(t, int):
            if t + ahead < heads:
                more()
            if t > 0:
                relay_step(t - 1)
        else:
            pl.when(t + ahead < heads)(more)
            relay_step(t - 1)

    def text_head(h, _):
        q = tq[:, :, :, :, col(h)].reshape(n * here, HD)
        scores = [qk(q, tiles[0, h, 0]), qk(q, tkv[core, side, row, 0, :, col(h)]) + bias_own]
        peak, total, acc = softmax_parts(scores, [tiles[0, h, 1], tkv[core, side, row, 1, :, col(h)]])
        part[:, :, :, :, col(h)] = acc.reshape(2, 2, nz, here, HD)
        lane = lax.broadcasted_iota(jnp.int32, (n * here, 128), 1) == h
        for base, value in ((width, peak), (width + 128, total)):
            old = part[:, :, :, :, base : base + 128].reshape(n * here, 128)
            new = jnp.where(lane, value, old)
            part[:, :, :, :, base : base + 128] = new.reshape(2, 2, nz, here, 128)
        return 0

    codes = []
    for j in range(listed.shape[1]):
        off = owner[listed[0, j]] - me
        code = jnp.where(off == sib - me, 3, 4)
        code = jnp.where(off == me - pair, 2, code)
        code = jnp.where(off == pair - me, 1, code)
        codes.append(jnp.where(off == 0, 0, code))
    hi_code = functools.reduce(jnp.maximum, codes)
    lo_code = sum(codes) - hi_code
    lo_far = lo_code == 2
    hi_sib = hi_code == 3
    hi_fwd = hi_code == 4

    def video_head(h):
        copy_s(h).wait_recv()

        @pl.when(relay_in)
        def _():
            copy_f(h).wait_recv()

        picked = []
        for j in range(2):
            near, far = tiles[1, h, j], tiles[2, h, j]
            lo = jnp.where(lo_far, far, near)
            hi = jnp.where(hi_fwd, tiles[4, h, j], jnp.where(hi_sib, tiles[3, h, j], far))
            words = tkv[:, :, :, j, :, col(h)].reshape(n * here, HD)
            picked.append((tiles[0, h, j], lo, hi, words))
        block = 128
        for r in range(rows // block):
            qr = q_ref[r * block : (r + 1) * block, col(h)]
            scores = [qk(qr, key) for key in picked[0]]
            scores[3] = scores[3] + bias_all
            _, total, acc = softmax_parts(scores, picked[1])
            out[r * block : (r + 1) * block, col(h)] = (acc / total).astype(jnp.bfloat16)

    def joined(first, second):
        peak1, peak2 = first[:, width : width + 128], second[:, width : width + 128]
        joint = jnp.maximum(peak1, peak2)
        f1, f2 = jnp.exp2((peak1 - joint) * C2), jnp.exp2((peak2 - joint) * C2)
        total = first[:, width + 128 :] * f1 + second[:, width + 128 :] * f2
        pieces = [
            first[:, h * HD : (h + 1) * HD] * f1[:, h : h + 1]
            + second[:, h * HD : (h + 1) * HD] * f2[:, h : h + 1]
            for h in range(heads)
        ]
        return pieces + [joint, total]

    def store_joined(view, pieces):
        for i, piece in enumerate(pieces):
            view[:, i * 128 : (i + 1) * 128] = piece

    def part_s():
        return remote(part.at[1 - core], got_sib, p_send.at[0], p_recv.at[0], sib)

    def part_y():
        return remote(sent_pair, got_pair, p_send.at[1], p_recv.at[1], pair)

    def part_ys():
        return remote(
            part.at[core, 1 - side, :, :, pl.ds(width, 256)],
            pair_stats,
            p_send.at[2],
            p_recv.at[2],
            pair,
        )

    def part_z(k):
        there = lax.rem(row + k + 1, nz)
        return remote(
            part.at[core, side, there], got_row.at[k], pz_send.at[k], pz_recv.at[k], peers[k]
        )

    def join_sib(i, _):
        y, z = i // nz, lax.rem(i, nz)
        store_joined(part.at[core, y, z], joined(part[core, y, z], got_sib[y, z]))
        return 0

    def round_pair(z, _):
        sent_pair[z] = part[core, 1 - side, z, :, :width].astype(jnp.bfloat16)
        return 0

    def join_pair(z, _):
        theirs = jnp.concatenate([got_pair[z].astype(jnp.float32), pair_stats[z]], axis=1)
        store_joined(part.at[core, side, z], joined(part[core, side, z], theirs))
        return 0

    for k in range(nz - 1):
        text_z_wait(tq, 0, k)
    text_y(tq, 0, True).start()
    pump(0)
    text_y(tq, 0, False).wait_recv()
    text_s(tq, 0, True).start()
    for k in range(nz - 1):
        text_z_wait(tkv, 1, k)
    text_y(tkv, 1, True).start()
    pump(1)
    text_s(tq, 0, False).wait_recv()
    half = heads // 2
    lax.fori_loop(0, half, text_head, 0)
    pump(2)
    lax.fori_loop(half, heads, text_head, 0)
    part_s().start()
    pump(3)
    text_y(tkv, 1, False).wait_recv()
    text_s(tkv, 1, True).start()
    part_s().wait_recv()
    lax.fori_loop(0, 2 * nz, join_sib, 0)
    lax.fori_loop(0, nz, round_pair, 0)
    part_y().start()
    part_ys().start()
    pump(4)
    text_s(tkv, 1, False).wait_recv()
    query_in.wait()

    def video_pair(i, _):
        pump(5 + i)
        lax.fori_loop(2 * i, 2 * i + 2, lambda h, c: (video_head(h), c)[1], 0)
        return 0

    lax.fori_loop(0, 3, video_pair, 0)
    part_y().wait_recv()
    part_ys().wait_recv()
    lax.fori_loop(0, nz, join_pair, 0)
    for k in range(nz - 1):
        part_z(k).start()

    def video_last(i, _):
        pump(8 + i)
        video_head(6 + i)
        return 0

    lax.fori_loop(0, heads - 8, video_last, 0)
    video_head(heads - 2)
    relay_step(heads - 1)
    whole = part[core, side, row]
    for k in range(nz - 1):
        part_z(k).wait_recv()
        whole = jnp.concatenate(joined(whole, got_row[k]), axis=1)
    for h in range(heads):
        total = whole[:, width + 128 + h : width + 129 + h]
        text_out[:, h * HD : (h + 1) * HD] = (whole[:, h * HD : (h + 1) * HD] / total).astype(
            jnp.bfloat16
        )
    video_head(heads - 1)

    for i, buf in enumerate((tq, tkv)):
        for k in range(nz - 1):
            text_z(buf, i, k).wait_send()
        text_y(buf, i, True).wait_send()
        text_s(buf, i, True).wait_send()
    part_s().wait_send()
    part_y().wait_send()
    part_ys().wait_send()
    for k in range(nz - 1):
        part_z(k).wait_send()

    def drain(h, _):
        copy_a(h).wait_send()
        copy_s(h).wait_send()

        @pl.when(has_to)
        def _():
            copy_b(h).wait_send()

        @pl.when(relay_ok)
        def _():
            copy_f(h).wait_send()

        return 0

    lax.fori_loop(0, heads, drain, 0)


def fused(qv, kv, vv, qt, kt, vt, key_tiles, tile_owner, text_count):
    n = lax.axis_size("ctx")
    rows, width = qv.shape
    heads = width // HD
    here = qt.shape[0]
    nz = n // 4
    vmem = pl.BlockSpec(memory_space=pltpu.VMEM)
    dma = pltpu.SemaphoreType.DMA
    wide = width + 256
    return pl.pallas_call(
        functools.partial(fused_kernel, n),
        in_specs=[pl.BlockSpec(memory_space=pltpu.SMEM)] * 3
        + [pl.BlockSpec(memory_space=pl.ANY)] * 6,
        out_specs=[vmem, vmem],
        out_shape=[
            jax.ShapeDtypeStruct((rows, width), jnp.bfloat16),
            jax.ShapeDtypeStruct((here, width), jnp.bfloat16),
        ],
        scratch_shapes=[
            pltpu.VMEM((rows, width), jnp.bfloat16),
            pltpu.VMEM((5, heads, 2, rows, HD), jnp.bfloat16),
            pltpu.VMEM((2, 2, nz, here, width), jnp.bfloat16),
            pltpu.VMEM((2, 2, nz, 2, here, width), jnp.bfloat16),
            pltpu.VMEM((2, 2, nz, here, wide), jnp.float32),
            pltpu.VMEM((2, nz, here, wide), jnp.float32),
            pltpu.VMEM((nz, here, width), jnp.bfloat16),
            pltpu.VMEM((nz, here, 256), jnp.float32),
            pltpu.VMEM((nz, here, width), jnp.bfloat16),
            pltpu.VMEM((nz - 1, here, wide), jnp.float32),
        ]
        + [dma((heads,))] * 8
        + [dma((2, nz - 1))] * 2
        + [dma((2, 2))] * 2
        + [dma((3,))] * 2
        + [dma((nz - 1,))] * 2
        + [dma((2, heads)), dma((4,))],
        compiler_params=pltpu.CompilerParams(
            collective_id=0, has_side_effects=True, vmem_limit_bytes=56 << 20
        ),
        name="tile_attention",
    )(key_tiles, tile_owner, text_count, qv, kv, vv, qt, kt, vt)


def whole_device(*args):
    n = lax.axis_size("ctx")
    rows, width = args[0].shape
    here = args[3].shape[0]
    if rows == TILE and n % 4 == 0 and n >= 8 and n & (n - 1) == 0 and here in (16, 32, 64) and width // HD == 12:
        return fused(*args)
    return on_device(*args)


def solution(mesh):
    split = P(("groups", "ctx"), None)
    return jax.shard_map(
        whole_device,
        mesh=mesh,
        in_specs=(split,) * 7 + (P("groups"), P("groups")),
        out_specs=(split, split),
        check_vma=False,
    )
```
